32 devices in a mesh: replica: 8 (over z, x), tensor: 4 (over y, core).
Axes of the slice: x: 2, y: 2, z: 4, core: 2. Of those that a mesh axis runs over, the one named last changes fastest.
Arguments:
- hidden_acts: bfloat16 [4096, 16384], P('replica', 'tensor'), may hold values from -6 to 6
- out_grad: bfloat16 [4096, 768], P('replica'), may hold values from -0.25 to 0.25
- error_prev: bfloat16 [8, 768, 16384], P('replica', None, 'tensor'), may hold values from -6 to 6
- right_prev: bfloat16 [16384, 128], P('tensor'), may hold values from -6 to 6
Outputs:
- error_next: bfloat16 [8, 768, 16384], P('replica', None, 'tensor')
- right_next: float32 [16384, 128], P('tensor')
The draws below stay inside these ranges and needn't reach their ends.
All inputs are finite; a program needn't handle non-finite values.
Results may differ from the reference program's by a relative error of at most 0.0058.
Values may be sent and summed in bfloat16 or wider, within the bound.
A program may use at most 64 MiB of HBM per device.

```python
import jax
import jax.numpy as jnp
from jax import lax

D = 768
FF = 16384
RANK = 128
TOK_DEV = 512
TOKENS = 4096
N_REPLICA = 8


def shard_levels(own_key, shape, split, least, largest):
    def one(axis_at, parts):
        heights = jax.random.uniform(jax.random.fold_in(jax.random.fold_in(own_key, 6), axis_at), (parts,), jnp.float32, least / len(split), largest / len(split))
        return jnp.repeat(jnp.exp(heights), shape[axis_at] // parts).reshape((-1,) + (1,) * (len(shape) - axis_at - 1))

    loudness = one(*split[0])
    for cut in split[1:]:
        loudness = loudness * one(*cut)
    return loudness


def noise(stream_key, extent, scale, limit, split=(), dtype=jnp.bfloat16):
    drawn = scale * jax.random.normal(stream_key, extent, jnp.float32)
    if split:
        drawn = drawn * shard_levels(stream_key, extent, split, -0.22, 0.18)
    return jnp.clip(drawn, -limit, limit).astype(dtype)


def setup_inputs(seed: int = 0) -> dict:
    arg_keys = jax.random.split(jax.random.key(seed), 5)
    hidden_acts = noise(arg_keys[0], (TOKENS, FF), 1.0, 6.0, ((0, 8), (1, 4)))
    out_grad = noise(arg_keys[1], (TOKENS, D), TOK_DEV ** -0.5, 0.25, ((0, 8),))
    error_prev = noise(arg_keys[2], (N_REPLICA, D, FF), 1.0, 6.0, ((0, 8), (2, 4)))
    right_prev = noise(arg_keys[3], (FF, RANK), 1.0, 6.0, ((0, 4),))
    return {"hidden_acts": hidden_acts, "out_grad": out_grad, "error_prev": error_prev, "right_prev": right_prev}


def compensate(acts, cot, err):
    grad = lax.dot_general(cot.astype(jnp.float32), acts.astype(jnp.float32), (((0,), (0,)), ((), ())), preferred_element_type=jnp.float32)
    return (grad + err.astype(jnp.float32)).astype(jnp.bfloat16)

def reference(hidden_acts, out_grad, error_prev, right_prev):
    acts = hidden_acts.reshape(N_REPLICA, TOK_DEV, FF)
    cots = out_grad.reshape(N_REPLICA, TOK_DEV, D)

    def left_term(carry, items):
        comp = compensate(items[0], items[1], items[2])
        return (carry + jnp.dot(comp.astype(jnp.float32), right_prev.astype(jnp.float32), preferred_element_type=jnp.float32), None)
    p_sum, unused = lax.scan(left_term, jnp.zeros((D, RANK), jnp.float32), (acts, cots, error_prev))
    gram_matrix = jnp.dot(p_sum.T, p_sum, precision=lax.Precision.HIGHEST)
    factor = jnp.linalg.cholesky(gram_matrix)
    left_low = jax.scipy.linalg.solve_triangular(factor, p_sum.T, lower=True).T.astype(jnp.bfloat16)

    def right_term(carry, items):
        comp = compensate(items[0], items[1], items[2])
        term = lax.dot_general(comp.astype(jnp.float32), left_low.astype(jnp.float32), (((0,), (0,)), ((), ())), preferred_element_type=jnp.float32)
        return (carry + term, None)
    right_total, unused = lax.scan(right_term, jnp.zeros((FF, RANK), jnp.float32), (acts, cots, error_prev))
    right_next = right_total / N_REPLICA
    right_low = right_next.astype(jnp.bfloat16)
    approx = lax.dot_general(left_low.astype(jnp.float32), right_low.astype(jnp.float32), (((1,), (1,)), ((), ())), preferred_element_type=jnp.float32)

    def new_error(items):
        comp = compensate(items[0], items[1], items[2])
        return (comp.astype(jnp.float32) - approx).astype(jnp.bfloat16)
    error_next = lax.map(new_error, (acts, cots, error_prev))
    return (error_next, right_next)
```

```python
import functools

import jax
import jax.numpy as jnp
from jax import lax
from jax.experimental import pallas as pl
from jax.experimental.pallas import tpu as pltpu
from jax.sharding import PartitionSpec as P

MESH = pl.DeviceIdType.MESH
VMEM = pl.BlockSpec(memory_space=pltpu.VMEM)


def wait_bytes(view, sem):
    pltpu.make_async_copy(view, view, sem).wait()


def left_kernel(replicas, tensors, piece, x_ref, out_ref, recv, mine, gathered, send_sem, recv_sem, send2_sem, recv2_sem):
    count = replicas * tensors
    me = lax.axis_index("replica") * tensors + lax.axis_index("tensor")

    def peer(k):
        other = lax.rem(me + k, count)
        return other, (other // tensors, lax.rem(other, tensors))

    barrier = pltpu.get_barrier_semaphore()

    def greet(k, carry):
        pl.semaphore_signal(barrier, inc=1, device_id=peer(k)[1], device_id_type=MESH)
        return carry

    lax.fori_loop(1, count, greet, 0)
    pl.semaphore_wait(barrier, count - 1)

    def scatter(k, carry):
        other, where = peer(k)
        pltpu.make_async_remote_copy(
            src_ref=x_ref.at[other], dst_ref=recv.at[k - 1], send_sem=send_sem, recv_sem=recv_sem,
            device_id=where, device_id_type=MESH,
        ).start()
        return carry

    lax.fori_loop(1, count, scatter, 0)
    wait_bytes(recv, recv_sem)
    mine[...] = x_ref[me] + jnp.sum(recv[...], axis=0)

    def gather(k, carry):
        other, where = peer(k)
        pltpu.make_async_remote_copy(
            src_ref=mine, dst_ref=gathered.at[me], send_sem=send2_sem, recv_sem=recv2_sem,
            device_id=where, device_id_type=MESH,
        ).start()
        return carry

    lax.fori_loop(1, count, gather, 0)
    gathered[me] = mine[...]
    wait_bytes(recv, recv2_sem)
    out_ref[...] = gathered[...]
    wait_bytes(recv, send_sem)
    wait_bytes(recv, send2_sem)


def left_sum(partial_value, replicas, tensors):
    rows, rank = partial_value.shape
    count = replicas * tensors
    piece = -(-rows // (count * 8)) * 8
    padded = jnp.pad(partial_value, ((0, count * piece - rows), (0, 0))).reshape(count, piece, rank)
    out = pl.pallas_call(
        functools.partial(left_kernel, replicas, tensors, piece),
        out_shape=jax.ShapeDtypeStruct((count, piece, rank), jnp.float32),
        in_specs=[VMEM],
        out_specs=VMEM,
        scratch_shapes=[
            pltpu.VMEM((count - 1, piece, rank), jnp.float32),
            pltpu.VMEM((piece, rank), jnp.float32),
            pltpu.VMEM((count, piece, rank), jnp.float32),
            pltpu.SemaphoreType.DMA, pltpu.SemaphoreType.DMA, pltpu.SemaphoreType.DMA, pltpu.SemaphoreType.DMA,
        ],
        compiler_params=pltpu.CompilerParams(collective_id=0, has_side_effects=True),
    )(padded)
    return out.reshape(count * piece, rank)[:rows]


def right_kernel(replicas, inner, chunks, x_ref, out_ref, sendx, recvx, sendz, recvz, final, gathz, gathx,
                 sx, rx, sz, rz, sg, rg, sh, rh):
    outer = replicas // inner
    me = lax.axis_index("replica")
    mz, mx = me // inner, lax.rem(me, inner)
    px = lax.rem(mx + 1, inner)
    partner = {"replica": mz * inner + px}

    def zpeer(k):
        oz = lax.rem(mz + k, outer)
        return oz, {"replica": oz * inner + mx}

    barrier = pltpu.get_barrier_semaphore()
    pl.semaphore_signal(barrier, inc=1, device_id=partner, device_id_type=MESH)
    for k in range(1, outer):
        pl.semaphore_signal(barrier, inc=1, device_id=zpeer(k)[1], device_id_type=MESH)
    pl.semaphore_wait(barrier, outer)

    for c in range(chunks):
        sendx[c] = x_ref[px, :, c].astype(jnp.bfloat16)
        if True:
            pltpu.make_async_remote_copy(
                src_ref=sendx.at[c], dst_ref=recvx.at[c], send_sem=sx.at[c], recv_sem=rx.at[c],
                device_id=partner, device_id_type=MESH,
            ).start()
    for c in range(chunks):
        wait_bytes(recvx.at[c], rx.at[c])
        sendz[c] = (x_ref[mx, :, c] + recvx[c].astype(jnp.float32)).astype(jnp.bfloat16)
        for k in range(1, outer):
            oz, where = zpeer(k)
            pltpu.make_async_remote_copy(
                src_ref=sendz.at[c, oz], dst_ref=recvz.at[c, k - 1], send_sem=sz.at[c], recv_sem=rz.at[c],
                device_id=where, device_id_type=MESH,
            ).start()
    for c in range(chunks):
        wait_bytes(recvz.at[c], rz.at[c])
        own = x_ref[mx, mz, c] + recvx[c, mz].astype(jnp.float32)
        total = own + jnp.sum(recvz[c].astype(jnp.float32), axis=0)
        final[c] = (total / replicas).astype(jnp.bfloat16)
        for k in range(1, outer):
            oz, where = zpeer(k)
            pltpu.make_async_remote_copy(
                src_ref=final.at[c], dst_ref=gathz.at[c, mz], send_sem=sg.at[c], recv_sem=rg.at[c],
                device_id=where, device_id_type=MESH,
            ).start()
        gathz[c, mz] = final[c]
    for c in range(chunks):
        wait_bytes(recvz.at[c], rg.at[c])
        pltpu.make_async_remote_copy(
            src_ref=gathz.at[c], dst_ref=gathx.at[c], send_sem=sh.at[c], recv_sem=rh.at[c],
            device_id=partner, device_id_type=MESH,
        ).start()
        out_ref[mx, :, c] = gathz[c]
    for c in range(chunks):
        wait_bytes(gathx.at[c], rh.at[c])
        out_ref[px, :, c] = gathx[c]
    for c in range(chunks):
        wait_bytes(sendx.at[c], sx.at[c])
        wait_bytes(recvz.at[c], sz.at[c])
        wait_bytes(recvz.at[c], sg.at[c])
        wait_bytes(gathz.at[c], sh.at[c])


def right_mean(terms, replicas):
    width, rank = terms.shape
    inner = 2
    outer = replicas // inner
    rows = width // replicas
    chunks = next(c for c in (4, 2, 1) if rows % (c * 16) == 0)
    rows //= chunks
    shape = (inner, outer, chunks, rows, rank)
    bf = jnp.bfloat16
    out = pl.pallas_call(
        functools.partial(right_kernel, replicas, inner, chunks),
        out_shape=jax.ShapeDtypeStruct(shape, bf),
        in_specs=[VMEM],
        out_specs=VMEM,
        scratch_shapes=[
            pltpu.VMEM((chunks, outer, rows, rank), bf),
            pltpu.VMEM((chunks, outer, rows, rank), bf),
            pltpu.VMEM((chunks, outer, rows, rank), bf),
            pltpu.VMEM((chunks, outer - 1, rows, rank), bf),
            pltpu.VMEM((chunks, rows, rank), bf),
            pltpu.VMEM((chunks, outer, rows, rank), bf),
            pltpu.VMEM((chunks, outer, rows, rank), bf),
        ] + [pltpu.SemaphoreType.DMA((chunks,))] * 8,
        compiler_params=pltpu.CompilerParams(collective_id=1, has_side_effects=True),
    )(terms.reshape(shape))
    return out.reshape(width, rank)


def orthonormal(p_rows, gram_matrix):
    factor = jnp.linalg.cholesky(gram_matrix)
    return jax.scipy.linalg.solve_triangular(factor, p_rows.T, lower=True).T.astype(jnp.bfloat16)


def shards(hidden_acts, out_grad, error_prev, right_prev):
    replicas, tensors = lax.axis_size("replica"), lax.axis_size("tensor")
    weight_grad = lax.dot_general(
        out_grad, hidden_acts, (((0,), (0,)), ((), ())), preferred_element_type=jnp.float32
    )
    compensated = (weight_grad + error_prev[0].astype(jnp.float32)).astype(jnp.bfloat16)
    partial_value = jnp.dot(compensated, right_prev, preferred_element_type=jnp.float32)
    p_sum = left_sum(partial_value, replicas, tensors)
    gram_matrix = jnp.dot(p_sum.T, p_sum, precision=lax.Precision.HIGHEST)
    left_low = orthonormal(p_sum, gram_matrix)
    right_terms = lax.dot_general(
        compensated, left_low, (((0,), (0,)), ((), ())), preferred_element_type=jnp.float32
    )
    right_low = right_mean(right_terms, replicas)
    right_next = right_low.astype(jnp.float32)
    approx = lax.dot_general(
        left_low, right_low, (((1,), (1,)), ((), ())), preferred_element_type=jnp.float32
    )
    error_next = (compensated.astype(jnp.float32) - approx).astype(jnp.bfloat16)
    return (error_next[None], right_next)


def solution(mesh):
    return jax.shard_map(
        shards,
        mesh=mesh,
        in_specs=(
            P("replica", "tensor"),
            P("replica", None),
            P("replica", None, "tensor"),
            P("tensor", None),
        ),
        out_specs=(P("replica", None, "tensor"), P("tensor", None)),
        check_vma=False,
    )
```

```python
import functools

import jax
import jax.numpy as jnp
from jax import lax
from jax.experimental import pallas as pl
from jax.experimental.pallas import tpu as pltpu
from jax.sharding import PartitionSpec as P

MESH = pl.DeviceIdType.MESH
VMEM = pl.BlockSpec(memory_space=pltpu.VMEM)


def wait_bytes(view, sem):
    pltpu.make_async_copy(view, view, sem).wait()


def left_kernel(replicas, tensors, piece, x_ref, out_ref, recv, mine, gathered, send_sem, recv_sem, send2_sem, recv2_sem):
    count = replicas * tensors
    me = lax.axis_index("replica") * tensors + lax.axis_index("tensor")

    def peer(k):
        other = lax.rem(me + k, count)
        return other, (other // tensors, lax.rem(other, tensors))

    barrier = pltpu.get_barrier_semaphore()

    def greet(k, carry):
        pl.semaphore_signal(barrier, inc=1, device_id=peer(k)[1], device_id_type=MESH)
        return carry

    lax.fori_loop(1, count, greet, 0)
    pl.semaphore_wait(barrier, count - 1)

    def scatter(k, carry):
        other, where = peer(k)
        pltpu.make_async_remote_copy(
            src_ref=x_ref.at[other], dst_ref=recv.at[k - 1], send_sem=send_sem, recv_sem=recv_sem,
            device_id=where, device_id_type=MESH,
        ).start()
        return carry

    lax.fori_loop(1, count, scatter, 0)
    wait_bytes(recv, recv_sem)
    mine[...] = x_ref[me] + jnp.sum(recv[...], axis=0)

    def gather(k, carry):
        other, where = peer(k)
        pltpu.make_async_remote_copy(
            src_ref=mine, dst_ref=gathered.at[me], send_sem=send2_sem, recv_sem=recv2_sem,
            device_id=where, device_id_type=MESH,
        ).start()
        return carry

    lax.fori_loop(1, count, gather, 0)
    gathered[me] = mine[...]
    wait_bytes(recv, recv2_sem)
    out_ref[...] = gathered[...]
    wait_bytes(recv, send_sem)
    wait_bytes(recv, send2_sem)


def left_sum(partial_value, replicas, tensors):
    rows, rank = partial_value.shape
    count = replicas * tensors
    piece = -(-rows // (count * 8)) * 8
    padded = jnp.pad(partial_value, ((0, count * piece - rows), (0, 0))).reshape(count, piece, rank)
    out = pl.pallas_call(
        functools.partial(left_kernel, replicas, tensors, piece),
        out_shape=jax.ShapeDtypeStruct((count, piece, rank), jnp.float32),
        in_specs=[VMEM],
        out_specs=VMEM,
        scratch_shapes=[
            pltpu.VMEM((count - 1, piece, rank), jnp.float32),
            pltpu.VMEM((piece, rank), jnp.float32),
            pltpu.VMEM((count, piece, rank), jnp.float32),
            pltpu.SemaphoreType.DMA, pltpu.SemaphoreType.DMA, pltpu.SemaphoreType.DMA, pltpu.SemaphoreType.DMA,
        ],
        compiler_params=pltpu.CompilerParams(collective_id=0, has_side_effects=True),
    )(padded)
    return out.reshape(count * piece, rank)[:rows]


def right_kernel(replicas, inner, chunks, x_ref, out_ref, sendx, recvx, sendz, recvz, final, gathz, gathx,
                 sx, rx, sz, rz, sg, rg, sh, rh):
    outer = replicas // inner
    me = lax.axis_index("replica")
    mz, mx = me // inner, lax.rem(me, inner)
    px = lax.rem(mx + 1, inner)
    partner = {"replica": mz * inner + px}

    def zpeer(k):
        oz = lax.rem(mz + k, outer)
        return oz, {"replica": oz * inner + mx}

    barrier = pltpu.get_barrier_semaphore()
    pl.semaphore_signal(barrier, inc=1, device_id=partner, device_id_type=MESH)
    for k in range(1, outer):
        pl.semaphore_signal(barrier, inc=1, device_id=zpeer(k)[1], device_id_type=MESH)
    pl.semaphore_wait(barrier, outer)

    for c in range(chunks):
        sendx[c] = x_ref[px, :, c].astype(jnp.bfloat16)
        if True:
            pltpu.make_async_remote_copy(
                src_ref=sendx.at[c], dst_ref=recvx.at[c], send_sem=sx.at[c], recv_sem=rx.at[c],
                device_id=partner, device_id_type=MESH,
            ).start()
    for c in range(chunks):
        wait_bytes(recvx.at[c], rx.at[c])
        sendz[c] = (x_ref[mx, :, c] + recvx[c].astype(jnp.float32)).astype(jnp.bfloat16)
        for k in range(1, outer):
            oz, where = zpeer(k)
            pltpu.make_async_remote_copy(
                src_ref=sendz.at[c, oz], dst_ref=recvz.at[c, k - 1], send_sem=sz.at[c], recv_sem=rz.at[c],
                device_id=where, device_id_type=MESH,
            ).start()
    for c in range(chunks):
        wait_bytes(recvz.at[c], rz.at[c])
        own = x_ref[mx, mz, c] + recvx[c, mz].astype(jnp.float32)
        total = own + jnp.sum(recvz[c].astype(jnp.float32), axis=0)
        final[c] = (total / replicas).astype(jnp.bfloat16)
        for k in range(1, outer):
            oz, where = zpeer(k)
            pltpu.make_async_remote_copy(
                src_ref=final.at[c], dst_ref=gathz.at[c, mz], send_sem=sg.at[c], recv_sem=rg.at[c],
                device_id=where, device_id_type=MESH,
            ).start()
        gathz[c, mz] = final[c]
    for c in range(chunks):
        wait_bytes(recvz.at[c], rg.at[c])
        pltpu.make_async_remote_copy(
            src_ref=gathz.at[c], dst_ref=gathx.at[c], send_sem=sh.at[c], recv_sem=rh.at[c],
            device_id=partner, device_id_type=MESH,
        ).start()
        out_ref[mx, :, c] = gathz[c]
    for c in range(chunks):
        wait_bytes(gathx.at[c], rh.at[c])
        out_ref[px, :, c] = gathx[c]
    for c in range(chunks):
        wait_bytes(sendx.at[c], sx.at[c])
        wait_bytes(recvz.at[c], sz.at[c])
        wait_bytes(recvz.at[c], sg.at[c])
        wait_bytes(gathz.at[c], sh.at[c])


def right_mean(terms, replicas):
    width, rank = terms.shape
    inner = 2
    outer = replicas // inner
    rows = width // replicas
    chunks = next(c for c in (4, 2, 1) if rows % (c * 16) == 0)
    rows //= chunks
    shape = (inner, outer, chunks, rows, rank)
    bf = jnp.bfloat16
    out = pl.pallas_call(
        functools.partial(right_kernel, replicas, inner, chunks),
        out_shape=jax.ShapeDtypeStruct(shape, bf),
        in_specs=[VMEM],
        out_specs=VMEM,
        scratch_shapes=[
            pltpu.VMEM((chunks, outer, rows, rank), bf),
            pltpu.VMEM((chunks, outer, rows, rank), bf),
            pltpu.VMEM((chunks, outer, rows, rank), bf),
            pltpu.VMEM((chunks, outer - 1, rows, rank), bf),
            pltpu.VMEM((chunks, rows, rank), bf),
            pltpu.VMEM((chunks, outer, rows, rank), bf),
            pltpu.VMEM((chunks, outer, rows, rank), bf),
        ] + [pltpu.SemaphoreType.DMA((chunks,))] * 8,
        compiler_params=pltpu.CompilerParams(collective_id=1, has_side_effects=True),
    )(terms.reshape(shape))
    return out.reshape(width, rank)


def inverse_factor(gram_matrix, block):
    rank = gram_matrix.shape[0]
    row = lax.broadcasted_iota(jnp.int32, (rank, rank), 0)
    col = lax.broadcasted_iota(jnp.int32, (rank, rank), 1)
    left = gram_matrix
    right = jnp.where(row == col, 1.0, 0.0).astype(jnp.float32)
    sub = lax.broadcasted_iota(jnp.int32, (block, rank), 0)
    done = []
    for start in range(0, rank, block):
        u, w = left[:block], right[:block]
        cols = [jnp.broadcast_to(u[:, start + j:start + j + 1], (block, rank)) for j in range(block)]
        scale = jnp.zeros((block, rank), jnp.float32)
        for j in range(block):
            pivot = cols[j][j:j + 1]
            scale = jnp.where(sub == j, lax.rsqrt(pivot), scale)
            m = jnp.where(sub > j, cols[j] * (1.0 / pivot), 0.0)
            for i in range(j + 1, block):
                cols[i] = cols[i] - m * cols[i][j:j + 1]
            u = u - m * u[j:j + 1]
            w = w - m * w[j:j + 1]
        u, w = u * scale, w * scale
        done.append(w)
        if start + block < rank:
            both = jnp.concatenate([u, w], axis=1)
            update = lax.dot_general(
                u, both, (((0,), (0,)), ((), ())), precision=lax.Precision.HIGHEST,
                preferred_element_type=jnp.float32,
            )[start + block:]
            left = left[block:] - update[:, :rank]
            right = right[block:] - update[:, rank:]
    return jnp.concatenate(done, axis=0)


def orthonormal_kernel(p_ref, out_ref):
    p = p_ref[...]
    gram_matrix = lax.dot_general(
        p, p, (((0,), (0,)), ((), ())), precision=lax.Precision.HIGHEST, preferred_element_type=jnp.float32
    )
    inverse = inverse_factor(gram_matrix, 16)
    out_ref[...] = lax.dot_general(
        p, inverse, (((1,), (1,)), ((), ())), precision=lax.Precision.HIGHEST, preferred_element_type=jnp.float32
    ).astype(out_ref.dtype)


def orthonormal(p_rows):
    return pl.pallas_call(
        orthonormal_kernel,
        out_shape=jax.ShapeDtypeStruct(p_rows.shape, jnp.bfloat16),
        in_specs=[VMEM],
        out_specs=VMEM,
    )(p_rows)


def shards(hidden_acts, out_grad, error_prev, right_prev):
    replicas, tensors = lax.axis_size("replica"), lax.axis_size("tensor")
    weight_grad = lax.dot_general(
        out_grad, hidden_acts, (((0,), (0,)), ((), ())), preferred_element_type=jnp.float32
    )
    compensated = (weight_grad + error_prev[0].astype(jnp.float32)).astype(jnp.bfloat16)
    partial_value = jnp.dot(compensated, right_prev, preferred_element_type=jnp.float32)
    p_sum = left_sum(partial_value, replicas, tensors)
    left_low = orthonormal(p_sum)
    right_terms = lax.dot_general(
        compensated, left_low, (((0,), (0,)), ((), ())), preferred_element_type=jnp.float32
    )
    right_low = right_mean(right_terms, replicas)
    right_next = right_low.astype(jnp.float32)
    approx = lax.dot_general(
        left_low, right_low, (((1,), (1,)), ((), ())), preferred_element_type=jnp.float32
    )
    error_next = (compensated.astype(jnp.float32) - approx).astype(jnp.bfloat16)
    return (error_next[None], right_next)


def solution(mesh):
    return jax.shard_map(
        shards,
        mesh=mesh,
        in_specs=(
            P("replica", "tensor"),
            P("replica", None),
            P("replica", None, "tensor"),
            P("tensor", None),
        ),
        out_specs=(P("replica", None, "tensor"), P("tensor", None)),
        check_vma=False,
    )
```

```python
import functools

import jax
import jax.numpy as jnp
from jax import lax
from jax.experimental import pallas as pl
from jax.experimental.pallas import tpu as pltpu
from jax.sharding import PartitionSpec as P

MESH = pl.DeviceIdType.MESH
VMEM = pl.BlockSpec(memory_space=pltpu.VMEM)


def wait_bytes(view, sem):
    pltpu.make_async_copy(view, view, sem).wait()


def left_kernel(replicas, tensors, piece, x_ref, out_ref, recv, mine, gathered, send_sem, recv_sem, send2_sem, recv2_sem):
    count = replicas * tensors
    me = lax.axis_index("replica") * tensors + lax.axis_index("tensor")

    def peer(k):
        other = lax.rem(me + k, count)
        return other, (other // tensors, lax.rem(other, tensors))

    barrier = pltpu.get_barrier_semaphore()

    def greet(k, carry):
        pl.semaphore_signal(barrier, inc=1, device_id=peer(k)[1], device_id_type=MESH)
        return carry

    lax.fori_loop(1, count, greet, 0)
    pl.semaphore_wait(barrier, count - 1)

    def scatter(k, carry):
        other, where = peer(k)
        pltpu.make_async_remote_copy(
            src_ref=x_ref.at[other], dst_ref=recv.at[k - 1], send_sem=send_sem, recv_sem=recv_sem,
            device_id=where, device_id_type=MESH,
        ).start()
        return carry

    lax.fori_loop(1, count, scatter, 0)
    wait_bytes(recv, recv_sem)
    mine[...] = x_ref[me] + jnp.sum(recv[...], axis=0)

    def gather(k, carry):
        other, where = peer(k)
        pltpu.make_async_remote_copy(
            src_ref=mine, dst_ref=gathered.at[me], send_sem=send2_sem, recv_sem=recv2_sem,
            device_id=where, device_id_type=MESH,
        ).start()
        return carry

    lax.fori_loop(1, count, gather, 0)
    gathered[me] = mine[...]
    wait_bytes(recv, recv2_sem)
    out_ref[...] = gathered[...]
    wait_bytes(recv, send_sem)
    wait_bytes(recv, send2_sem)


def left_sum(partial_value, replicas, tensors):
    rows, rank = partial_value.shape
    count = replicas * tensors
    piece = -(-rows // (count * 8)) * 8
    padded = jnp.pad(partial_value, ((0, count * piece - rows), (0, 0))).reshape(count, piece, rank)
    out = pl.pallas_call(
        functools.partial(left_kernel, replicas, tensors, piece),
        out_shape=jax.ShapeDtypeStruct((count, piece, rank), jnp.float32),
        in_specs=[VMEM],
        out_specs=VMEM,
        scratch_shapes=[
            pltpu.VMEM((count - 1, piece, rank), jnp.float32),
            pltpu.VMEM((piece, rank), jnp.float32),
            pltpu.VMEM((count, piece, rank), jnp.float32),
            pltpu.SemaphoreType.DMA, pltpu.SemaphoreType.DMA, pltpu.SemaphoreType.DMA, pltpu.SemaphoreType.DMA,
        ],
        compiler_params=pltpu.CompilerParams(collective_id=0, has_side_effects=True),
    )(padded)
    return out.reshape(count * piece, rank)[:rows]


def right_kernel(replicas, inner, chunks, rows, comp_hbm, left_ref, out_ref, comp, sendx, recvx, own, sendz, recvz,
                 final, gathz, gathx, load, sx, rx, sz, rz, sg, rg, sh, rh):
    outer = replicas // inner
    rank = left_ref.shape[1]
    slab = outer * rows
    me = lax.axis_index("replica")
    mz, mx = me // inner, lax.rem(me, inner)
    px = lax.rem(mx + 1, inner)
    partner = {"replica": mz * inner + px}

    def fetch(side, c):
        start = pl.multiple_of((side * chunks + c) * slab, slab)
        place = c if side is px else chunks + c
        return pltpu.make_async_copy(comp_hbm.at[:, pl.ds(start, slab)], comp.at[place], load.at[place])

    for c in range(chunks):
        fetch(px, c).start()
    for c in range(chunks):
        fetch(mx, c).start()

    def terms(side, c):
        fetch(side, c).wait()
        place = c if side is px else chunks + c
        return lax.dot_general(
            comp[place], left_ref[...], (((0,), (0,)), ((), ())), preferred_element_type=jnp.float32
        ).reshape(outer, rows, rank)

    def zpeer(k):
        oz = lax.rem(mz + k, outer)
        return oz, {"replica": oz * inner + mx}

    barrier = pltpu.get_barrier_semaphore()
    pl.semaphore_signal(barrier, inc=1, device_id=partner, device_id_type=MESH)
    for k in range(1, outer):
        pl.semaphore_signal(barrier, inc=1, device_id=zpeer(k)[1], device_id_type=MESH)

    def pair_scatter(c):
        sendx[c] = terms(px, c).astype(jnp.bfloat16)
        if c == 0:
            pl.semaphore_wait(barrier, outer)
        pltpu.make_async_remote_copy(
            src_ref=sendx.at[c], dst_ref=recvx.at[c], send_sem=sx.at[c], recv_sem=rx.at[c],
            device_id=partner, device_id_type=MESH,
        ).start()

    def line_scatter(c):
        mine = terms(mx, c)
        wait_bytes(recvx.at[c], rx.at[c])
        own[c] = mine + recvx[c].astype(jnp.float32)
        sendz[c] = own[c].astype(jnp.bfloat16)
        for k in range(1, outer):
            oz, where = zpeer(k)
            pltpu.make_async_remote_copy(
                src_ref=sendz.at[c, oz], dst_ref=recvz.at[c, k - 1], send_sem=sz.at[c], recv_sem=rz.at[c],
                device_id=where, device_id_type=MESH,
            ).start()

    def line_gather(c):
        wait_bytes(recvz.at[c], rz.at[c])
        total = own[c, mz] + jnp.sum(recvz[c].astype(jnp.float32), axis=0)
        final[c] = (total / replicas).astype(jnp.bfloat16)
        for k in range(1, outer):
            oz, where = zpeer(k)
            pltpu.make_async_remote_copy(
                src_ref=final.at[c], dst_ref=gathz.at[c, mz], send_sem=sg.at[c], recv_sem=rg.at[c],
                device_id=where, device_id_type=MESH,
            ).start()
        gathz[c, mz] = final[c]

    def pair_gather(c):
        wait_bytes(recvz.at[c], rg.at[c])
        pltpu.make_async_remote_copy(
            src_ref=gathz.at[c], dst_ref=gathx.at[c], send_sem=sh.at[c], recv_sem=rh.at[c],
            device_id=partner, device_id_type=MESH,
        ).start()
        out_ref[mx, c] = gathz[c]

    for c in range(chunks):
        pair_scatter(c)
    lag = 3
    for step in range(chunks + 2 * lag):
        if step < chunks:
            line_scatter(step)
        if 0 <= step - lag < chunks:
            line_gather(step - lag)
        if 0 <= step - 2 * lag < chunks:
            pair_gather(step - 2 * lag)
    for c in range(chunks):
        wait_bytes(gathx.at[c], rh.at[c])
        out_ref[px, c] = gathx[c]
    for c in range(chunks):
        wait_bytes(sendx.at[c], sx.at[c])
        wait_bytes(recvz.at[c], sz.at[c])
        wait_bytes(recvz.at[c], sg.at[c])
        wait_bytes(gathz.at[c], sh.at[c])


def right_mean(compensated, left_low, replicas):
    depth, width = compensated.shape
    rank = left_low.shape[1]
    inner = 2
    outer = replicas // inner
    piece = width // replicas
    chunks = next(c for c in (8, 4, 2, 1) if piece % (c * 16) == 0 and (width // inner // c) % 128 == 0)
    rows = piece // chunks
    bf = jnp.bfloat16
    whole = pltpu.VMEM((chunks, outer, rows, rank), bf)
    out = pl.pallas_call(
        functools.partial(right_kernel, replicas, inner, chunks, rows),
        out_shape=jax.ShapeDtypeStruct((inner, chunks, outer, rows, rank), bf),
        in_specs=[pl.BlockSpec(memory_space=pl.ANY), VMEM],
        out_specs=VMEM,
        scratch_shapes=[
            pltpu.VMEM((inner * chunks, depth, outer * rows), bf),
            whole,
            whole,
            pltpu.VMEM((chunks, outer, rows, rank), jnp.float32),
            whole,
            pltpu.VMEM((chunks, outer - 1, rows, rank), bf),
            pltpu.VMEM((chunks, rows, rank), bf),
            whole,
            whole,
            pltpu.SemaphoreType.DMA((inner * chunks,)),
        ] + [pltpu.SemaphoreType.DMA((chunks,))] * 8,
        compiler_params=pltpu.CompilerParams(collective_id=1, has_side_effects=True),
    )(compensated, left_low)
    return out.reshape(width, rank)


def inverse_factor(gram_matrix, block):
    rank = gram_matrix.shape[0]
    row = lax.broadcasted_iota(jnp.int32, (rank, rank), 0)
    col = lax.broadcasted_iota(jnp.int32, (rank, rank), 1)
    left = gram_matrix
    right = jnp.where(row == col, 1.0, 0.0).astype(jnp.float32)
    sub = lax.broadcasted_iota(jnp.int32, (block, rank), 0)
    done = []
    for start in range(0, rank, block):
        u, w = left[:block], right[:block]
        cols = [jnp.broadcast_to(u[:, start + j:start + j + 1], (block, rank)) for j in range(block)]
        scale = jnp.zeros((block, rank), jnp.float32)
        for j in range(block):
            pivot = cols[j][j:j + 1]
            scale = jnp.where(sub == j, lax.rsqrt(pivot), scale)
            m = jnp.where(sub > j, cols[j] * (1.0 / pivot), 0.0)
            for i in range(j + 1, block):
                cols[i] = cols[i] - m * cols[i][j:j + 1]
            u = u - m * u[j:j + 1]
            w = w - m * w[j:j + 1]
        u, w = u * scale, w * scale
        done.append(w)
        if start + block < rank:
            both = jnp.concatenate([u, w], axis=1)
            update = lax.dot_general(
                u, both, (((0,), (0,)), ((), ())), precision=lax.Precision.HIGHEST,
                preferred_element_type=jnp.float32,
            )[start + block:]
            left = left[block:] - update[:, :rank]
            right = right[block:] - update[:, rank:]
    return jnp.concatenate(done, axis=0)


def orthonormal_kernel(p_ref, out_ref):
    p = p_ref[...]
    gram_matrix = lax.dot_general(
        p, p, (((0,), (0,)), ((), ())), precision=lax.Precision.HIGHEST, preferred_element_type=jnp.float32
    )
    inverse = inverse_factor(gram_matrix, 16)
    out_ref[...] = lax.dot_general(
        p, inverse, (((1,), (1,)), ((), ())), precision=lax.Precision.HIGHEST, preferred_element_type=jnp.float32
    ).astype(out_ref.dtype)


def orthonormal(p_rows):
    return pl.pallas_call(
        orthonormal_kernel,
        out_shape=jax.ShapeDtypeStruct(p_rows.shape, jnp.bfloat16),
        in_specs=[VMEM],
        out_specs=VMEM,
    )(p_rows)


def shards(hidden_acts, out_grad, error_prev, right_prev):
    replicas, tensors = lax.axis_size("replica"), lax.axis_size("tensor")
    weight_grad = lax.dot_general(
        out_grad, hidden_acts, (((0,), (0,)), ((), ())), preferred_element_type=jnp.float32
    )
    compensated = (weight_grad + error_prev[0].astype(jnp.float32)).astype(jnp.bfloat16)
    partial_value = jnp.dot(compensated, right_prev, preferred_element_type=jnp.float32)
    p_sum = left_sum(partial_value, replicas, tensors)
    left_low = orthonormal(p_sum)
    right_low = right_mean(compensated, left_low, replicas)
    right_next = right_low.astype(jnp.float32)
    approx = lax.dot_general(
        left_low, right_low, (((1,), (1,)), ((), ())), preferred_element_type=jnp.float32
    )
    error_next = (compensated.astype(jnp.float32) - approx).astype(jnp.bfloat16)
    return (error_next[None], right_next)


def solution(mesh):
    return jax.shard_map(
        shards,
        mesh=mesh,
        in_specs=(
            P("replica", "tensor"),
            P("replica", None),
            P("replica", None, "tensor"),
            P("tensor", None),
        ),
        out_specs=(P("replica", None, "tensor"), P("tensor", None)),
        check_vma=False,
    )
```

```python
import functools

import jax
import jax.numpy as jnp
from jax import lax
from jax.experimental import pallas as pl
from jax.experimental.pallas import tpu as pltpu
from jax.sharding import PartitionSpec as P

MESH = pl.DeviceIdType.MESH
VMEM = pl.BlockSpec(memory_space=pltpu.VMEM)


def wait_bytes(view, sem):
    pltpu.make_async_copy(view, view, sem).wait()


def left_kernel(replicas, tensors, chunks, tiles, used, act_hbm, cot_hbm, err_hbm, right_hbm, comp_hbm, out_ref,
                act, cot, err, right, comp, part, half, recvc, recv, mine, gathered, other,
                act_sem, cot_sem, err_sem, right_sem, comp_sem, sc, rc, ss, rs, sg, rg, sh, rh):
    lines = tensors // 2
    peers = replicas * lines
    rows = cot.shape[1] // chunks
    width = act.shape[2]
    replica, tensor = lax.axis_index("replica"), lax.axis_index("tensor")
    core = lax.rem(tensor, 2)
    mate = 1 - core
    partner = (replica, tensor - core + mate)
    me = replica * lines + tensor // 2

    def peer(k):
        q = lax.rem(me + k, peers)
        return q, (q // lines, lax.rem(q, lines) * 2 + core)

    def err_copy(c, t):
        return pltpu.make_async_copy(
            err_hbm.at[0, pl.ds(c * rows, rows), pl.ds(t * width, width)], err.at[c, t], err_sem.at[c, t])

    def comp_copy(c, t):
        return pltpu.make_async_copy(
            comp.at[c, t], comp_hbm.at[pl.ds(c * rows, rows), pl.ds(t * width, width)], comp_sem.at[c, t])

    def act_copy(t):
        return pltpu.make_async_copy(act_hbm.at[:, pl.ds(t * width, width)], act.at[t], act_sem.at[t])

    def right_copy(t):
        return pltpu.make_async_copy(right_hbm.at[pl.ds(t * width, width)], right.at[t], right_sem.at[t])

    pltpu.make_async_copy(cot_hbm, cot, cot_sem).start()
    for t in range(tiles):
        act_copy(t).start()
        err_copy(0, t).start()
        right_copy(t).start()
    for c in range(1, chunks):
        for t in range(tiles):
            err_copy(c, t).start()

    barrier = pltpu.get_barrier_semaphore()
    pl.semaphore_signal(barrier, inc=1, device_id=partner, device_id_type=MESH)

    def greet(k, carry):
        pl.semaphore_signal(barrier, inc=1, device_id=peer(k)[1], device_id_type=MESH)
        return carry

    lax.fori_loop(1, peers, greet, 0)

    def core_copy(c):
        return pltpu.make_async_remote_copy(
            src_ref=part.at[c, mate], dst_ref=recvc.at[c], send_sem=sc.at[c], recv_sem=rc.at[c],
            device_id=partner, device_id_type=MESH,
        )

    def scatter_chunk(c):
        wait_bytes(recvc.at[c], rc.at[c])
        half[c, :used] = (part[c, core] + recvc[c]).reshape(half[c, :used].shape)
        if used < peers:
            half[c, used:] = jnp.zeros_like(half[c, used:])

        def scatter(k, carry):
            q, where = peer(k)
            pltpu.make_async_remote_copy(
                src_ref=half.at[c, q], dst_ref=recv.at[k - 1, c], send_sem=ss, recv_sem=rs,
                device_id=where, device_id_type=MESH,
            ).start()
            return carry

        lax.fori_loop(1, peers, scatter, 0)

    for c in range(chunks):
        total = jnp.zeros((rows, right.shape[2]), jnp.float32)
        for t in range(tiles):
            if c == 0:
                if t == 0:
                    pltpu.make_async_copy(cot_hbm, cot, cot_sem).wait()
                act_copy(t).wait()
                right_copy(t).wait()
            err_copy(c, t).wait()
            grad = lax.dot_general(
                cot[:, c * rows:(c + 1) * rows], act[t], (((0,), (0,)), ((), ())),
                preferred_element_type=jnp.float32,
            )
            compensated = (grad + err[c, t].astype(jnp.float32)).astype(jnp.bfloat16)
            comp[c, t] = compensated
            comp_copy(c, t).start()
            total = total + jnp.dot(compensated, right[t], preferred_element_type=jnp.float32)
        part[c] = total.reshape(part.shape[1:])
        if c == 0:
            pl.semaphore_wait(barrier, peers)
        core_copy(c).start()
        if c:
            scatter_chunk(c - 1)
    scatter_chunk(chunks - 1)

    wait_bytes(recv, rs)
    mine[...] = half[:, me] + jnp.sum(recv[...], axis=0)

    def gather(k, carry):
        q, where = peer(k)
        pltpu.make_async_remote_copy(
            src_ref=mine, dst_ref=gathered.at[me], send_sem=sg, recv_sem=rg,
            device_id=where, device_id_type=MESH,
        ).start()
        return carry

    lax.fori_loop(1, peers, gather, 0)
    gathered[me] = mine[...]
    wait_bytes(recv, rg)
    pltpu.make_async_remote_copy(
        src_ref=gathered, dst_ref=other, send_sem=sh, recv_sem=rh, device_id=partner, device_id_type=MESH,
    ).start()
    for c in range(chunks):
        out_ref[c, core] = gathered[:used, c]
    wait_bytes(other, rh)
    for c in range(chunks):
        out_ref[c, mate] = other[:used, c]
    for c in range(chunks):
        wait_bytes(part.at[c, mate], sc.at[c])
        for t in range(tiles):
            comp_copy(c, t).wait()
    wait_bytes(recv, ss)
    wait_bytes(recv, sg)
    wait_bytes(gathered, sh)


def left_sum(hidden_acts, out_grad, error_prev, right_prev, replicas, tensors):
    tokens, depth = out_grad.shape
    columns, rank = right_prev.shape
    peers = replicas * tensors // 2
    chunks = next(c for c in (3, 2, 1) if depth % (c * 256) == 0)
    tiles = next(t for t in (4, 2, 1) if columns % (t * 128) == 0)
    rows, width = depth // chunks, columns // tiles
    piece = -(-rows // (2 * peers * 8)) * 8
    used = rows // (2 * piece)
    bf, f32, dma = jnp.bfloat16, jnp.float32, pltpu.SemaphoreType.DMA
    hbm = pl.BlockSpec(memory_space=pl.ANY)
    compensated, p_sum = pl.pallas_call(
        functools.partial(left_kernel, replicas, tensors, chunks, tiles, used),
        out_shape=(
            jax.ShapeDtypeStruct((depth, columns), bf),
            jax.ShapeDtypeStruct((chunks, 2, used, piece, rank), f32),
        ),
        in_specs=[hbm] * 4,
        out_specs=(hbm, VMEM),
        scratch_shapes=[
            pltpu.VMEM((tiles, tokens, width), bf),
            pltpu.VMEM((tokens, depth), bf),
            pltpu.VMEM((chunks, tiles, rows, width), bf),
            pltpu.VMEM((tiles, width, rank), bf),
            pltpu.VMEM((chunks, tiles, rows, width), bf),
            pltpu.VMEM((chunks, 2, rows // 2, rank), f32),
            pltpu.VMEM((chunks, peers, piece, rank), f32),
            pltpu.VMEM((chunks, rows // 2, rank), f32),
            pltpu.VMEM((peers - 1, chunks, piece, rank), f32),
            pltpu.VMEM((chunks, piece, rank), f32),
            pltpu.VMEM((peers, chunks, piece, rank), f32),
            pltpu.VMEM((peers, chunks, piece, rank), f32),
            dma((tiles,)), dma, dma((chunks, tiles)), dma((tiles,)), dma((chunks, tiles)),
            dma((chunks,)), dma((chunks,)), dma, dma, dma, dma, dma, dma,
        ],
        compiler_params=pltpu.CompilerParams(collective_id=0, has_side_effects=True),
    )(hidden_acts, out_grad, error_prev, right_prev)
    return compensated, p_sum.reshape(depth, rank)


def right_kernel(replicas, inner, chunks, rows, comp_hbm, left_ref, out_ref, comp, sendx, recvx, own, sendz, recvz,
                 final, gathz, gathx, load, sx, rx, sz, rz, sg, rg, sh, rh):
    outer = replicas // inner
    rank = left_ref.shape[1]
    slab = outer * rows
    me = lax.axis_index("replica")
    mz, mx = me // inner, lax.rem(me, inner)
    px = lax.rem(mx + 1, inner)
    partner = {"replica": mz * inner + px}

    def fetch(side, c):
        start = pl.multiple_of((side * chunks + c) * slab, slab)
        place = c if side is px else chunks + c
        return pltpu.make_async_copy(comp_hbm.at[:, pl.ds(start, slab)], comp.at[place], load.at[place])

    for c in range(chunks):
        fetch(px, c).start()
    for c in range(chunks):
        fetch(mx, c).start()

    def terms(side, c):
        fetch(side, c).wait()
        place = c if side is px else chunks + c
        return lax.dot_general(
            comp[place], left_ref[...], (((0,), (0,)), ((), ())), preferred_element_type=jnp.float32
        ).reshape(outer, rows, rank)

    def zpeer(k):
        oz = lax.rem(mz + k, outer)
        return oz, {"replica": oz * inner + mx}

    barrier = pltpu.get_barrier_semaphore()
    pl.semaphore_signal(barrier, inc=1, device_id=partner, device_id_type=MESH)
    for k in range(1, outer):
        pl.semaphore_signal(barrier, inc=1, device_id=zpeer(k)[1], device_id_type=MESH)

    def pair_scatter(c):
        sendx[c] = terms(px, c).astype(jnp.bfloat16)
        if c == 0:
            pl.semaphore_wait(barrier, outer)
        pltpu.make_async_remote_copy(
            src_ref=sendx.at[c], dst_ref=recvx.at[c], send_sem=sx.at[c], recv_sem=rx.at[c],
            device_id=partner, device_id_type=MESH,
        ).start()

    def line_scatter(c):
        mine = terms(mx, c)
        wait_bytes(recvx.at[c], rx.at[c])
        own[c] = mine + recvx[c].astype(jnp.float32)
        sendz[c] = own[c].astype(jnp.bfloat16)
        for k in range(1, outer):
            oz, where = zpeer(k)
            pltpu.make_async_remote_copy(
                src_ref=sendz.at[c, oz], dst_ref=recvz.at[c, k - 1], send_sem=sz.at[c], recv_sem=rz.at[c],
                device_id=where, device_id_type=MESH,
            ).start()

    def line_gather(c):
        wait_bytes(recvz.at[c], rz.at[c])
        total = own[c, mz] + jnp.sum(recvz[c].astype(jnp.float32), axis=0)
        final[c] = (total / replicas).astype(jnp.bfloat16)
        for k in range(1, outer):
            oz, where = zpeer(k)
            pltpu.make_async_remote_copy(
                src_ref=final.at[c], dst_ref=gathz.at[c, mz], send_sem=sg.at[c], recv_sem=rg.at[c],
                device_id=where, device_id_type=MESH,
            ).start()
        gathz[c, mz] = final[c]

    def pair_gather(c):
        wait_bytes(recvz.at[c], rg.at[c])
        pltpu.make_async_remote_copy(
            src_ref=gathz.at[c], dst_ref=gathx.at[c], send_sem=sh.at[c], recv_sem=rh.at[c],
            device_id=partner, device_id_type=MESH,
        ).start()
        out_ref[mx, c] = gathz[c]

    for c in range(chunks):
        pair_scatter(c)
    lag = 3
    for step in range(chunks + 2 * lag):
        if step < chunks:
            line_scatter(step)
        if 0 <= step - lag < chunks:
            line_gather(step - lag)
        if 0 <= step - 2 * lag < chunks:
            pair_gather(step - 2 * lag)
    for c in range(chunks):
        wait_bytes(gathx.at[c], rh.at[c])
        out_ref[px, c] = gathx[c]
    for c in range(chunks):
        wait_bytes(sendx.at[c], sx.at[c])
        wait_bytes(recvz.at[c], sz.at[c])
        wait_bytes(recvz.at[c], sg.at[c])
        wait_bytes(gathz.at[c], sh.at[c])


def right_mean(compensated, left_low, replicas):
    depth, width = compensated.shape
    rank = left_low.shape[1]
    inner = 2
    outer = replicas // inner
    piece = width // replicas
    chunks = next(c for c in (8, 4, 2, 1) if piece % (c * 16) == 0 and (width // inner // c) % 128 == 0)
    rows = piece // chunks
    bf = jnp.bfloat16
    whole = pltpu.VMEM((chunks, outer, rows, rank), bf)
    out = pl.pallas_call(
        functools.partial(right_kernel, replicas, inner, chunks, rows),
        out_shape=jax.ShapeDtypeStruct((inner, chunks, outer, rows, rank), bf),
        in_specs=[pl.BlockSpec(memory_space=pl.ANY), VMEM],
        out_specs=VMEM,
        scratch_shapes=[
            pltpu.VMEM((inner * chunks, depth, outer * rows), bf),
            whole,
            whole,
            pltpu.VMEM((chunks, outer, rows, rank), jnp.float32),
            whole,
            pltpu.VMEM((chunks, outer - 1, rows, rank), bf),
            pltpu.VMEM((chunks, rows, rank), bf),
            whole,
            whole,
            pltpu.SemaphoreType.DMA((inner * chunks,)),
        ] + [pltpu.SemaphoreType.DMA((chunks,))] * 8,
        compiler_params=pltpu.CompilerParams(collective_id=1, has_side_effects=True),
    )(compensated, left_low)
    return out.reshape(width, rank)


def inverse_factor(gram_matrix, block):
    rank = gram_matrix.shape[0]
    row = lax.broadcasted_iota(jnp.int32, (rank, rank), 0)
    col = lax.broadcasted_iota(jnp.int32, (rank, rank), 1)
    left = gram_matrix
    right = jnp.where(row == col, 1.0, 0.0).astype(jnp.float32)
    sub = lax.broadcasted_iota(jnp.int32, (block, rank), 0)
    done = []
    for start in range(0, rank, block):
        u, w = left[:block], right[:block]
        cols = [jnp.broadcast_to(u[:, start + j:start + j + 1], (block, rank)) for j in range(block)]
        scale = jnp.zeros((block, rank), jnp.float32)
        for j in range(block):
            pivot = cols[j][j:j + 1]
            scale = jnp.where(sub == j, lax.rsqrt(pivot), scale)
            m = jnp.where(sub > j, cols[j] * (1.0 / pivot), 0.0)
            for i in range(j + 1, block):
                cols[i] = cols[i] - m * cols[i][j:j + 1]
            u = u - m * u[j:j + 1]
            w = w - m * w[j:j + 1]
        u, w = u * scale, w * scale
        done.append(w)
        if start + block < rank:
            both = jnp.concatenate([u, w], axis=1)
            update = lax.dot_general(
                u, both, (((0,), (0,)), ((), ())), precision=lax.Precision.HIGHEST,
                preferred_element_type=jnp.float32,
            )[start + block:]
            left = left[block:] - update[:, :rank]
            right = right[block:] - update[:, rank:]
    return jnp.concatenate(done, axis=0)


def orthonormal_kernel(p_ref, out_ref):
    p = p_ref[...]
    gram_matrix = lax.dot_general(
        p, p, (((0,), (0,)), ((), ())), precision=lax.Precision.HIGHEST, preferred_element_type=jnp.float32
    )
    inverse = inverse_factor(gram_matrix, 16)
    out_ref[...] = lax.dot_general(
        p, inverse, (((1,), (1,)), ((), ())), precision=lax.Precision.HIGHEST, preferred_element_type=jnp.float32
    ).astype(out_ref.dtype)


def orthonormal(p_rows):
    return pl.pallas_call(
        orthonormal_kernel,
        out_shape=jax.ShapeDtypeStruct(p_rows.shape, jnp.bfloat16),
        in_specs=[VMEM],
        out_specs=VMEM,
    )(p_rows)


def shards(hidden_acts, out_grad, error_prev, right_prev):
    replicas, tensors = lax.axis_size("replica"), lax.axis_size("tensor")
    compensated, p_sum = left_sum(hidden_acts, out_grad, error_prev, right_prev, replicas, tensors)
    left_low = orthonormal(p_sum)
    right_low = right_mean(compensated, left_low, replicas)
    right_next = right_low.astype(jnp.float32)
    approx = lax.dot_general(
        left_low, right_low, (((1,), (1,)), ((), ())), preferred_element_type=jnp.float32
    )
    error_next = (compensated.astype(jnp.float32) - approx).astype(jnp.bfloat16)
    return (error_next[None], right_next)


def solution(mesh):
    return jax.shard_map(
        shards,
        mesh=mesh,
        in_specs=(
            P("replica", "tensor"),
            P("replica", None),
            P("replica", None, "tensor"),
            P("tensor", None),
        ),
        out_specs=(P("replica", None, "tensor"), P("tensor", None)),
        check_vma=False,
    )
```

```python
import functools

import jax
import jax.numpy as jnp
from jax import lax
from jax.experimental import pallas as pl
from jax.experimental.pallas import tpu as pltpu
from jax.sharding import PartitionSpec as P

MESH = pl.DeviceIdType.MESH
VMEM = pl.BlockSpec(memory_space=pltpu.VMEM)


def wait_bytes(view, sem):
    pltpu.make_async_copy(view, view, sem).wait()


def left_kernel(replicas, tensors, chunks, tiles, used, act_hbm, cot_hbm, err_hbm, right_hbm, comp_hbm, out_ref,
                act, cot, err, right, comp, part, half, recvc, recv, mine, gathered, other,
                act_sem, cot_sem, err_sem, right_sem, comp_sem, sc, rc, ss, rs, sg, rg, sh, rh):
    lines = tensors // 2
    peers = replicas * lines
    rows = cot.shape[1] // chunks
    width = act.shape[2]
    replica, tensor = lax.axis_index("replica"), lax.axis_index("tensor")
    core = lax.rem(tensor, 2)
    mate = 1 - core
    partner = (replica, tensor - core + mate)
    me = replica * lines + tensor // 2

    def peer(k):
        q = lax.rem(me + k, peers)
        return q, (q // lines, lax.rem(q, lines) * 2 + core)

    def err_copy(c, t):
        return pltpu.make_async_copy(
            err_hbm.at[0, pl.ds(c * rows, rows), pl.ds(t * width, width)], err.at[c, t], err_sem.at[c, t])

    def comp_copy(c, t):
        return pltpu.make_async_copy(
            comp.at[c, t], comp_hbm.at[pl.ds(c * rows, rows), pl.ds(t * width, width)], comp_sem.at[c, t])

    def act_copy(t):
        return pltpu.make_async_copy(act_hbm.at[:, pl.ds(t * width, width)], act.at[t], act_sem.at[t])

    def right_copy(t):
        return pltpu.make_async_copy(right_hbm.at[pl.ds(t * width, width)], right.at[t], right_sem.at[t])

    pltpu.make_async_copy(cot_hbm, cot, cot_sem).start()
    for t in range(tiles):
        act_copy(t).start()
        err_copy(0, t).start()
        right_copy(t).start()
    for c in range(1, chunks):
        for t in range(tiles):
            err_copy(c, t).start()

    barrier = pltpu.get_barrier_semaphore()
    pl.semaphore_signal(barrier, inc=1, device_id=partner, device_id_type=MESH)

    def greet(k, carry):
        pl.semaphore_signal(barrier, inc=1, device_id=peer(k)[1], device_id_type=MESH)
        return carry

    lax.fori_loop(1, peers, greet, 0)

    def core_copy(c):
        return pltpu.make_async_remote_copy(
            src_ref=part.at[c, mate], dst_ref=recvc.at[c], send_sem=sc.at[c], recv_sem=rc.at[c],
            device_id=partner, device_id_type=MESH,
        )

    def scatter_chunk(c):
        wait_bytes(recvc.at[c], rc.at[c])
        half[c, :used] = (part[c, core] + recvc[c]).reshape(half[c, :used].shape)
        if used < peers:
            half[c, used:] = jnp.zeros_like(half[c, used:])

        def scatter(k, carry):
            q, where = peer(k)
            pltpu.make_async_remote_copy(
                src_ref=half.at[c, q], dst_ref=recv.at[k - 1, c], send_sem=ss, recv_sem=rs,
                device_id=where, device_id_type=MESH,
            ).start()
            return carry

        lax.fori_loop(1, peers, scatter, 0)

    for c in range(chunks):
        total = jnp.zeros((rows, right.shape[2]), jnp.float32)
        for t in range(tiles):
            if c == 0:
                if t == 0:
                    pltpu.make_async_copy(cot_hbm, cot, cot_sem).wait()
                act_copy(t).wait()
                right_copy(t).wait()
            err_copy(c, t).wait()
            grad = lax.dot_general(
                cot[:, c * rows:(c + 1) * rows], act[t], (((0,), (0,)), ((), ())),
                preferred_element_type=jnp.float32,
            )
            compensated = (grad + err[c, t].astype(jnp.float32)).astype(jnp.bfloat16)
            comp[c, t] = compensated
            comp_copy(c, t).start()
            total = total + jnp.dot(compensated, right[t], preferred_element_type=jnp.float32)
        part[c] = total.reshape(part.shape[1:])
        if c == 0:
            pl.semaphore_wait(barrier, peers)
        core_copy(c).start()
        if c:
            scatter_chunk(c - 1)
    scatter_chunk(chunks - 1)

    wait_bytes(recv, rs)
    mine[...] = half[:, me] + jnp.sum(recv[...], axis=0)

    def gather(k, carry):
        q, where = peer(k)
        pltpu.make_async_remote_copy(
            src_ref=mine, dst_ref=gathered.at[me], send_sem=sg, recv_sem=rg,
            device_id=where, device_id_type=MESH,
        ).start()
        return carry

    lax.fori_loop(1, peers, gather, 0)
    gathered[me] = mine[...]
    wait_bytes(recv, rg)
    pltpu.make_async_remote_copy(
        src_ref=gathered, dst_ref=other, send_sem=sh, recv_sem=rh, device_id=partner, device_id_type=MESH,
    ).start()
    for c in range(chunks):
        out_ref[c, core] = gathered[:used, c]
    wait_bytes(other, rh)
    for c in range(chunks):
        out_ref[c, mate] = other[:used, c]
    for c in range(chunks):
        wait_bytes(part.at[c, mate], sc.at[c])
        for t in range(tiles):
            comp_copy(c, t).wait()
    wait_bytes(recv, ss)
    wait_bytes(recv, sg)
    wait_bytes(gathered, sh)


def left_sum(hidden_acts, out_grad, error_prev, right_prev, replicas, tensors):
    tokens, depth = out_grad.shape
    columns, rank = right_prev.shape
    peers = replicas * tensors // 2
    chunks = next(c for c in (3, 2, 1) if depth % (c * 256) == 0)
    tiles = next(t for t in (4, 2, 1) if columns % (t * 128) == 0)
    rows, width = depth // chunks, columns // tiles
    piece = -(-rows // (2 * peers * 8)) * 8
    used = rows // (2 * piece)
    bf, f32, dma = jnp.bfloat16, jnp.float32, pltpu.SemaphoreType.DMA
    hbm = pl.BlockSpec(memory_space=pl.ANY)
    compensated, p_sum = pl.pallas_call(
        functools.partial(left_kernel, replicas, tensors, chunks, tiles, used),
        out_shape=(
            jax.ShapeDtypeStruct((depth, columns), bf),
            jax.ShapeDtypeStruct((chunks, 2, used, piece, rank), f32),
        ),
        in_specs=[hbm] * 4,
        out_specs=(hbm, VMEM),
        scratch_shapes=[
            pltpu.VMEM((tiles, tokens, width), bf),
            pltpu.VMEM((tokens, depth), bf),
            pltpu.VMEM((chunks, tiles, rows, width), bf),
            pltpu.VMEM((tiles, width, rank), bf),
            pltpu.VMEM((chunks, tiles, rows, width), bf),
            pltpu.VMEM((chunks, 2, rows // 2, rank), f32),
            pltpu.VMEM((chunks, peers, piece, rank), f32),
            pltpu.VMEM((chunks, rows // 2, rank), f32),
            pltpu.VMEM((peers - 1, chunks, piece, rank), f32),
            pltpu.VMEM((chunks, piece, rank), f32),
            pltpu.VMEM((peers, chunks, piece, rank), f32),
            pltpu.VMEM((peers, chunks, piece, rank), f32),
            dma((tiles,)), dma, dma((chunks, tiles)), dma((tiles,)), dma((chunks, tiles)),
            dma((chunks,)), dma((chunks,)), dma, dma, dma, dma, dma, dma,
        ],
        compiler_params=pltpu.CompilerParams(collective_id=0, has_side_effects=True, vmem_limit_bytes=60 * 1024 * 1024),
    )(hidden_acts, out_grad, error_prev, right_prev)
    return compensated, p_sum.reshape(depth, rank)


def right_kernel(replicas, inner, chunks, rows, comp_hbm, left_ref, out_ref, comp, sendx, recvx, own, sendz, recvz,
                 final, gathz, gathx, load, sx, rx, sz, rz, sg, rg, sh, rh):
    outer = replicas // inner
    rank = left_ref.shape[1]
    slab = outer * rows
    me = lax.axis_index("replica")
    mz, mx = me // inner, lax.rem(me, inner)
    px = lax.rem(mx + 1, inner)
    partner = {"replica": mz * inner + px}

    def fetch(side, c):
        start = pl.multiple_of((side * chunks + c) * slab, slab)
        place = c if side is px else chunks + c
        return pltpu.make_async_copy(comp_hbm.at[:, pl.ds(start, slab)], comp.at[place], load.at[place])

    for c in range(chunks):
        fetch(px, c).start()
    for c in range(chunks):
        fetch(mx, c).start()

    def terms(side, c):
        fetch(side, c).wait()
        place = c if side is px else chunks + c
        return lax.dot_general(
            comp[place], left_ref[...], (((0,), (0,)), ((), ())), preferred_element_type=jnp.float32
        ).reshape(outer, rows, rank)

    def zpeer(k):
        oz = lax.rem(mz + k, outer)
        return oz, {"replica": oz * inner + mx}

    barrier = pltpu.get_barrier_semaphore()
    pl.semaphore_signal(barrier, inc=1, device_id=partner, device_id_type=MESH)
    for k in range(1, outer):
        pl.semaphore_signal(barrier, inc=1, device_id=zpeer(k)[1], device_id_type=MESH)

    def pair_scatter(c):
        sendx[c] = terms(px, c).astype(jnp.bfloat16)
        if c == 0:
            pl.semaphore_wait(barrier, outer)
        pltpu.make_async_remote_copy(
            src_ref=sendx.at[c], dst_ref=recvx.at[c], send_sem=sx.at[c], recv_sem=rx.at[c],
            device_id=partner, device_id_type=MESH,
        ).start()

    def line_scatter(c):
        mine = terms(mx, c)
        wait_bytes(recvx.at[c], rx.at[c])
        own[c] = mine + recvx[c].astype(jnp.float32)
        sendz[c] = own[c].astype(jnp.bfloat16)
        for k in range(1, outer):
            oz, where = zpeer(k)
            pltpu.make_async_remote_copy(
                src_ref=sendz.at[c, oz], dst_ref=recvz.at[c, k - 1], send_sem=sz.at[c], recv_sem=rz.at[c],
                device_id=where, device_id_type=MESH,
            ).start()

    def line_gather(c):
        wait_bytes(recvz.at[c], rz.at[c])
        total = own[c, mz] + jnp.sum(recvz[c].astype(jnp.float32), axis=0)
        final[c] = (total / replicas).astype(jnp.bfloat16)
        for k in range(1, outer):
            oz, where = zpeer(k)
            pltpu.make_async_remote_copy(
                src_ref=final.at[c], dst_ref=gathz.at[c, mz], send_sem=sg.at[c], recv_sem=rg.at[c],
                device_id=where, device_id_type=MESH,
            ).start()
        gathz[c, mz] = final[c]

    def pair_gather(c):
        wait_bytes(recvz.at[c], rg.at[c])
        pltpu.make_async_remote_copy(
            src_ref=gathz.at[c], dst_ref=gathx.at[c], send_sem=sh.at[c], recv_sem=rh.at[c],
            device_id=partner, device_id_type=MESH,
        ).start()
        out_ref[mx, c] = gathz[c]

    for c in range(chunks):
        pair_scatter(c)
    lag = 4
    for step in range(chunks + 2 * lag):
        if step < chunks:
            line_scatter(step)
        if 0 <= step - lag < chunks:
            line_gather(step - lag)
        if 0 <= step - 2 * lag < chunks:
            pair_gather(step - 2 * lag)
    for c in range(chunks):
        wait_bytes(gathx.at[c], rh.at[c])
        out_ref[px, c] = gathx[c]
    for c in range(chunks):
        wait_bytes(sendx.at[c], sx.at[c])
        wait_bytes(recvz.at[c], sz.at[c])
        wait_bytes(recvz.at[c], sg.at[c])
        wait_bytes(gathz.at[c], sh.at[c])


def right_mean(compensated, left_low, replicas):
    depth, width = compensated.shape
    rank = left_low.shape[1]
    inner = 2
    outer = replicas // inner
    piece = width // replicas
    chunks = next(c for c in (8, 4, 2, 1) if piece % (c * 16) == 0 and (width // inner // c) % 128 == 0)
    rows = piece // chunks
    bf = jnp.bfloat16
    whole = pltpu.VMEM((chunks, outer, rows, rank), bf)
    out = pl.pallas_call(
        functools.partial(right_kernel, replicas, inner, chunks, rows),
        out_shape=jax.ShapeDtypeStruct((inner, chunks, outer, rows, rank), bf),
        in_specs=[pl.BlockSpec(memory_space=pl.ANY), VMEM],
        out_specs=VMEM,
        scratch_shapes=[
            pltpu.VMEM((inner * chunks, depth, outer * rows), bf),
            whole,
            whole,
            pltpu.VMEM((chunks, outer, rows, rank), jnp.float32),
            whole,
            pltpu.VMEM((chunks, outer - 1, rows, rank), bf),
            pltpu.VMEM((chunks, rows, rank), bf),
            whole,
            whole,
            pltpu.SemaphoreType.DMA((inner * chunks,)),
        ] + [pltpu.SemaphoreType.DMA((chunks,))] * 8,
        compiler_params=pltpu.CompilerParams(collective_id=1, has_side_effects=True, vmem_limit_bytes=54 * 1024 * 1024),
    )(compensated, left_low)
    return out.reshape(width, rank)


def inverse_factor(gram_matrix, block):
    rank = gram_matrix.shape[0]
    row = lax.broadcasted_iota(jnp.int32, (rank, rank), 0)
    col = lax.broadcasted_iota(jnp.int32, (rank, rank), 1)
    left = gram_matrix
    right = jnp.where(row == col, 1.0, 0.0).astype(jnp.float32)
    sub = lax.broadcasted_iota(jnp.int32, (block, rank), 0)
    done = []
    for start in range(0, rank, block):
        u, w = left[:block], right[:block]
        cols = [jnp.broadcast_to(u[:, start + j:start + j + 1], (block, rank)) for j in range(block)]
        scale = jnp.zeros((block, rank), jnp.float32)
        for j in range(block):
            pivot = cols[j][j:j + 1]
            scale = jnp.where(sub == j, lax.rsqrt(pivot), scale)
            m = jnp.where(sub > j, cols[j] * (1.0 / pivot), 0.0)
            for i in range(j + 1, block):
                cols[i] = cols[i] - m * cols[i][j:j + 1]
            u = u - m * u[j:j + 1]
            w = w - m * w[j:j + 1]
        u, w = u * scale, w * scale
        done.append(w)
        if start + block < rank:
            both = jnp.concatenate([u, w], axis=1)
            update = lax.dot_general(
                u, both, (((0,), (0,)), ((), ())), precision=lax.Precision.HIGHEST,
                preferred_element_type=jnp.float32,
            )[start + block:]
            left = left[block:] - update[:, :rank]
            right = right[block:] - update[:, rank:]
    return jnp.concatenate(done, axis=0)


def orthonormal_kernel(p_ref, out_ref):
    p = p_ref[...]
    gram_matrix = lax.dot_general(
        p, p, (((0,), (0,)), ((), ())), precision=lax.Precision.HIGHEST, preferred_element_type=jnp.float32
    )
    inverse = inverse_factor(gram_matrix, 32)
    out_ref[...] = lax.dot_general(
        p, inverse, (((1,), (1,)), ((), ())), precision=lax.Precision.HIGHEST, preferred_element_type=jnp.float32
    ).astype(out_ref.dtype)


def orthonormal(p_rows):
    return pl.pallas_call(
        orthonormal_kernel,
        out_shape=jax.ShapeDtypeStruct(p_rows.shape, jnp.bfloat16),
        in_specs=[VMEM],
        out_specs=VMEM,
        compiler_params=pltpu.CompilerParams(vmem_limit_bytes=16 * 1024 * 1024),
    )(p_rows)


def shards(hidden_acts, out_grad, error_prev, right_prev):
    replicas, tensors = lax.axis_size("replica"), lax.axis_size("tensor")
    compensated, p_sum = left_sum(hidden_acts, out_grad, error_prev, right_prev, replicas, tensors)
    left_low = orthonormal(p_sum)
    right_low = right_mean(compensated, left_low, replicas)
    right_next = right_low.astype(jnp.float32)
    approx = lax.dot_general(
        left_low, right_low, (((1,), (1,)), ((), ())), preferred_element_type=jnp.float32
    )
    error_next = (compensated.astype(jnp.float32) - approx).astype(jnp.bfloat16)
    return (error_next[None], right_next)


def solution(mesh):
    return jax.shard_map(
        shards,
        mesh=mesh,
        in_specs=(
            P("replica", "tensor"),
            P("replica", None),
            P("replica", None, "tensor"),
            P("tensor", None),
        ),
        out_specs=(P("replica", None, "tensor"), P("tensor", None)),
        check_vma=False,
    )
```
